512 devices in a mesh: section: 8 (over x, core), expert: 64 (over z, y).
Axes of the slice: x: 4, y: 8, z: 8, core: 2. Of those that a mesh axis runs over, the one named last changes fastest.
Arguments:
- x_fwd: bfloat16 [8, 8192, 3584], P('section', 'expert'), may hold values from -6 to 6
- routes_fwd: int32 [8, 8192, 8], P('section', 'expert'), may hold values from 0 to 255, as said below
- gates_fwd: float32 [8, 8192, 8], P('section', 'expert'), may hold values from 0.1 to 0.6
- w_gate: bfloat16 [8, 64, 3584, 128], P('section', 'expert'), may hold values from -0.09375 to 0.09375
- w_up: bfloat16 [8, 64, 3584, 128], P('section', 'expert'), may hold values from -0.09375 to 0.09375
- w_down: bfloat16 [8, 64, 128, 3584], P('section', 'expert'), may hold values from -0.1875 to 0.1875
Outputs:
- act_next: bfloat16 [8, 8192, 3584], P('section', 'expert')
The draws below stay inside these ranges and needn't reach their ends.
Inputs may be any that keep to these rules, and one draw needn't show every extreme that they name: `routes_fwd`: the 8 experts of a token differ. Within the rows of one device no expert below 8 is chosen by more than 10 tokens, and in every draw one such expert is chosen by exactly 10 tokens of every device.
All inputs are finite; a program needn't handle non-finite values.
Results may differ from the reference program's by a relative error of at most 0.0024.
Values may be sent and summed in bfloat16 or wider, within the bound.
No kernel may reach another device: no remote copies, remote signals or barrier semaphores. Data moves between devices by JAX's collectives and lax.ppermute only.
A program may use at most 64 MiB of HBM per device.

```python
import jax
import jax.numpy as jnp
from jax import lax

D = 3584
HID = 1024
H_DEV = 128
EXPERTS = 256
TOPK = 8
CAP = 10
TOK_DEV = 128
GROUP = 8
LIVE = 8
TOKENS = 8192
N_SECTION = 8
N_EXPERT = 64


def routes_law(key):
    blocks = N_SECTION * N_EXPERT
    key_list = jax.random.split(key, 6)
    hot_expert = jax.random.randint(key_list[0], (), 0, LIVE)
    live_ids = jnp.arange(LIVE, dtype=jnp.int32)
    levels = jax.random.randint(key_list[1], (LIVE,), 0, 2)
    levels = jnp.where(live_ids == hot_expert, 0, levels)
    counts = jax.random.randint(key_list[2], (blocks, LIVE), 0, CAP + 1)
    counts = jnp.right_shift(counts, levels[None, :])
    counts = jnp.where(live_ids[None, :] == hot_expert, CAP, counts)
    order_keys = jax.random.split(key_list[3], blocks * LIVE)
    orders = jax.vmap(lambda one_key: jax.random.permutation(one_key, TOK_DEV))(order_keys)
    rank_of = jnp.argsort(orders, axis=1).reshape(blocks, LIVE, TOK_DEV)
    chosen = (rank_of < counts[:, :, None]).astype(jnp.int32)
    chosen = jnp.transpose(chosen, (0, 2, 1))
    slot_of = jnp.cumsum(chosen, axis=2) - 1
    live_count = jnp.sum(chosen, axis=2)
    pick_cols = jnp.arange(TOPK, dtype=jnp.int32)
    hit = (chosen[:, :, :, None] == 1) & (slot_of[:, :, :, None] == pick_cols[None, None, None, :])
    live_list = jnp.sum(jnp.where(hit, live_ids[None, None, :, None], 0), axis=2)
    dead_keys = jax.random.split(key_list[4], blocks * TOK_DEV)
    dead_ids = jax.vmap(lambda one_key: jax.random.permutation(one_key, EXPERTS - LIVE)[:TOPK])(dead_keys)
    dead_ids = dead_ids.reshape(blocks, TOK_DEV, TOPK) + LIVE
    merged = jnp.where(pick_cols[None, None, :] < live_count[:, :, None], live_list, dead_ids)
    col_keys = jax.random.split(key_list[5], blocks * TOK_DEV)
    col_order = jax.vmap(lambda one_key: jax.random.permutation(one_key, TOPK))(col_keys)
    col_order = col_order.reshape(blocks, TOK_DEV, TOPK)
    shuffled = jnp.take_along_axis(merged, col_order, axis=2)
    return shuffled.reshape(N_SECTION, N_EXPERT * TOK_DEV, TOPK).astype(jnp.int32)


def draw_routes_fwd(key, part):
    return routes_law(jax.random.fold_in(key, 11))


def level_of(key, shape, cuts, least, top_value):
    def one(dim, parts):
        draws = jax.random.uniform(jax.random.fold_in(jax.random.fold_in(key, 6), dim), (parts,), jnp.float32, least / len(cuts), top_value / len(cuts))
        return jnp.repeat(jnp.exp(draws), shape[dim] // parts).reshape((-1,) + (1,) * (len(shape) - dim - 1))

    level = one(*cuts[0])
    for cut in cuts[1:]:
        level = level * one(*cut)
    return level


def bell_draw(key, shape, width, bound, pieces=(), kind=jnp.bfloat16):
    gain = level_of(key, shape, pieces, -0.22, 0.18) if pieces else 1.0
    array = jax.random.normal(key, shape, jnp.float32) * width * gain
    return jnp.minimum(jnp.maximum(array, -bound), bound).astype(kind)


def setup_inputs(seed: int = 0) -> dict:
    key_of = jax.random.split(jax.random.key(seed), 7)
    x_fwd = bell_draw(key_of[0], (N_SECTION, TOKENS, D), 1.0, 6.0, ((0, 8), (1, 64)))
    routes_fwd = draw_routes_fwd(jax.random.fold_in(key_of[6], 71), 0)
    gates_fwd = jnp.clip(0.1 + 0.5 * jax.random.uniform(key_of[2], (N_SECTION, TOKENS, TOPK), jnp.float32) ** level_of(key_of[2], (N_SECTION, TOKENS, TOPK), ((0, 8), (1, 64)), -0.2, 0.2), 0.1, 0.6)
    w_gate = bell_draw(key_of[3], (N_SECTION, LIVE * GROUP, D, H_DEV), D ** -0.5, 0.09375, ((0, 8), (1, 64)))
    w_up = bell_draw(key_of[4], (N_SECTION, LIVE * GROUP, D, H_DEV), D ** -0.5, 0.09375, ((0, 8), (1, 64)))
    w_down = bell_draw(key_of[5], (N_SECTION, LIVE * GROUP, H_DEV, D), HID ** -0.5, 0.1875, ((0, 8), (1, 64)))
    return dict(x_fwd=x_fwd, routes_fwd=routes_fwd, gates_fwd=gates_fwd, w_gate=w_gate, w_up=w_up, w_down=w_down)


def slot_index(routes):
    blocks = routes.reshape(N_EXPERT, TOK_DEV * TOPK)
    live_ids = jnp.arange(LIVE, dtype=jnp.int32)

    def place(block):
        onehot = (block[:, None] == live_ids[None, :]).astype(jnp.int32)
        before = jnp.cumsum(onehot, axis=0) - onehot
        return jnp.sum(onehot * before, axis=1).astype(jnp.int32)

    placed = jax.vmap(place)(blocks)
    source = jnp.arange(N_EXPERT, dtype=jnp.int32)[:, None]
    index = blocks * (N_EXPERT * CAP) + source * CAP + placed
    index = jnp.where(blocks < LIVE, index, LIVE * N_EXPERT * CAP)
    return index.reshape(TOKENS, TOPK).astype(jnp.int32)


def scatter_rows(rows, index):
    copies = jnp.broadcast_to(rows[:, None, :], (TOKENS, TOPK, D)).reshape(TOKENS * TOPK, D)
    buffer = jnp.zeros((LIVE * N_EXPERT * CAP + 1, D), jnp.bfloat16)
    buffer = buffer.at[index.reshape(-1)].set(copies)
    return buffer[:-1].reshape(LIVE, N_EXPERT * CAP, D)


def expert_forward(rows, wg, wu, wd):
    total = jnp.zeros((rows.shape[0], D), jnp.float32)
    for block in range(GROUP):
        pre_gate = jnp.dot(rows, wg[block], preferred_element_type=jnp.float32)
        pre_up = jnp.dot(rows, wu[block], preferred_element_type=jnp.float32)
        act = (pre_gate * jax.nn.sigmoid(pre_gate) * pre_up).astype(jnp.bfloat16)
        part = jnp.dot(act, wd[block], preferred_element_type=jnp.float32).astype(jnp.bfloat16)
        total = total + part.astype(jnp.float32)
    return total


def one_section(args):
    xa, ra, ga, wg, wu, wd = args
    wg = wg.reshape(LIVE, GROUP, D, H_DEV)
    wu = wu.reshape(LIVE, GROUP, D, H_DEV)
    wd = wd.reshape(LIVE, GROUP, H_DEV, D)
    index_a = slot_index(ra)
    slots_a = scatter_rows(xa, index_a)
    outs_a = lax.map(lambda z: expert_forward(z[0], z[1], z[2], z[3]), (slots_a, wg, wu, wd))
    flat = outs_a.reshape(LIVE * N_EXPERT * CAP, D)
    padded = jnp.concatenate([flat, jnp.zeros((1, D), jnp.float32)], axis=0)
    total = xa.astype(jnp.float32)
    for k in range(TOPK):
        total = total + ga[:, k][:, None] * padded[index_a[:, k]]
    return total.astype(jnp.bfloat16)


def reference(x_fwd, routes_fwd, gates_fwd, w_gate, w_up, w_down):
    y = lax.map(one_section, (x_fwd, routes_fwd, gates_fwd, w_gate, w_up, w_down))
    empty = jnp.zeros((1, TOKENS, D), jnp.bfloat16)
    return jnp.concatenate([empty, y[:-1]], axis=0)
```

```python
import functools

import jax
import jax.numpy as jnp
from jax import lax
from jax.experimental import pallas as pl
from jax.experimental.pallas import tpu as pltpu
from jax.sharding import Mesh, PartitionSpec as P

CAP = 10
LIVE = 8
PIECES = 4
BLOCK = CAP * PIECES
ROWS = LIVE * CAP
PLACED = LIVE * BLOCK

F32 = jnp.float32
BF16 = jnp.bfloat16


def iota(shape, dim):
    return lax.broadcasted_iota(jnp.int32, shape, dim)


def slot_keys(routes_t):
    tokens = routes_t.shape[1]
    hit = jnp.concatenate(
        [jnp.max((routes_t == e).astype(F32), axis=0, keepdims=True) for e in range(LIVE)], axis=0
    )
    earlier = (iota((tokens, tokens), 0) < iota((tokens, tokens), 1)).astype(BF16)
    rank = jnp.dot(hit.astype(BF16), earlier, preferred_element_type=F32)
    return jnp.where(hit > 0, rank, -1.0)


def spread(values):
    pick = (iota((PLACED, LIVE), 0) // BLOCK == iota((PLACED, LIVE), 1)).astype(BF16)
    return jnp.dot(pick, values, preferred_element_type=F32)


def slot_match(routes_t):
    keys = spread(slot_keys(routes_t).astype(BF16))
    slots = (iota(keys.shape, 0) % CAP).astype(F32)
    return keys == slots


def piece_of(shape):
    return iota(shape, 0) // CAP % PIECES


def place_kernel(routes_ref, x_ref, out_ref):
    match = slot_match(routes_ref[...])
    piece = piece_of(match.shape)
    width = x_ref.shape[1] // PIECES
    total = jnp.zeros(out_ref.shape, F32)
    for p in range(PIECES):
        one = jnp.where(match & (piece == p), 1.0, 0.0).astype(BF16)
        total += jnp.dot(one, x_ref[:, p * width:(p + 1) * width], preferred_element_type=F32)
    out_ref[...] = total.astype(BF16)


def whole_rows_kernel(in_ref, out_ref):
    width = in_ref.shape[1]
    row, col = iota((ROWS, PLACED), 0), iota((ROWS, PLACED), 1)
    same = (row // CAP == col // BLOCK) & (row % CAP == col % CAP)
    for p in range(PIECES):
        one = jnp.where(same & (col // CAP % PIECES == p), 1.0, 0.0).astype(BF16)
        moved = jnp.dot(one, in_ref[...], preferred_element_type=F32)
        out_ref[:, p * width:(p + 1) * width] = moved.astype(BF16)


def pieces_kernel(in_ref, out_ref):
    width = out_ref.shape[1]
    row, col = iota((PLACED, ROWS), 0), iota((PLACED, ROWS), 1)
    same = (col // CAP == row // BLOCK) & (col % CAP == row % CAP)
    total = jnp.zeros(out_ref.shape, F32)
    for p in range(PIECES):
        one = jnp.where(same & (row // CAP % PIECES == p), 1.0, 0.0).astype(BF16)
        total += jnp.dot(one, in_ref[:, p * width:(p + 1) * width], preferred_element_type=F32)
    out_ref[...] = total.astype(BF16)


def expert_kernel(rows_ref, wg_ref, wu_ref, wd_ref, out_ref, both_ref):
    hid = wg_ref.shape[1]

    @pl.when(pl.program_id(0) == 0)
    def _():
        both_ref[:, :hid] = wg_ref[...]
        both_ref[:, hid:] = wu_ref[...]

    pre = jnp.dot(rows_ref[...], both_ref[...], preferred_element_type=F32)
    gate, up = pre[:, :hid], pre[:, hid:]
    act = (gate * jax.nn.sigmoid(gate) * up).astype(BF16)
    out_ref[...] = jnp.dot(act, wd_ref[...], preferred_element_type=F32).astype(BF16)


def combine_kernel(routes_ref, gates_ref, x_ref, back_ref, out_ref):
    routes = routes_ref[...]
    match = slot_match(routes)
    gates = gates_ref[...]
    rows = [
        jnp.sum(jnp.where(routes == e, gates, 0.0), axis=0, keepdims=True) for e in range(LIVE)
    ]
    left = jnp.concatenate(rows, axis=0)
    terms = []
    for _ in range(3):
        term = left.astype(BF16)
        left = left - term.astype(F32)
        terms.append(jnp.where(match, spread(term), 0.0).astype(BF16))
    piece = piece_of(match.shape)
    width = back_ref.shape[1]
    back = back_ref[...]
    over_rows = (((0,), (0,)), ((), ()))
    for p in range(PIECES):
        here = piece == p
        total = x_ref[:, p * width:(p + 1) * width].astype(F32)
        for term in terms:
            one = jnp.where(here, term, jnp.zeros_like(term))
            total += lax.dot_general(one, back, over_rows, preferred_element_type=F32)
        out_ref[:, p * width:(p + 1) * width] = total.astype(BF16)


def whole(kernel, shape, *args):
    return pl.pallas_call(kernel, out_shape=jax.ShapeDtypeStruct(shape, BF16))(*args)


def expert_block(rows, wg, wu, wd):
    count, depth = rows.shape
    hid = wg.shape[1]
    tile = 128
    fixed = functools.partial(pl.BlockSpec, index_map=lambda i: (0, 0))
    return pl.pallas_call(
        expert_kernel,
        grid=(count // tile,),
        in_specs=[
            pl.BlockSpec((tile, depth), lambda i: (i, 0)),
            fixed((depth, hid)),
            fixed((depth, hid)),
            fixed((hid, depth)),
        ],
        out_specs=pl.BlockSpec((tile, depth), lambda i: (i, 0)),
        out_shape=jax.ShapeDtypeStruct((count, depth), BF16),
        scratch_shapes=[pltpu.VMEM((depth, 2 * hid), BF16)],
    )(rows, wg, wu, wd)


def shards(x_fwd, routes_fwd, gates_fwd, w_gate, w_up, w_down):
    x = x_fwd[0]
    routes_t, gates_t = routes_fwd[0].T, gates_fwd[0].T
    depth = x.shape[1]
    width = depth // PIECES
    placed = whole(place_kernel, (PLACED, width), routes_t, x)
    arrived = lax.all_to_all(placed.reshape(LIVE, BLOCK, width), "z", 0, 0, tiled=True)
    rows = whole(whole_rows_kernel, (ROWS, depth), arrived.reshape(PLACED, width))
    rows = lax.all_gather(rows, "y", axis=0, tiled=True)
    parts = expert_block(rows, w_gate[0, 0], w_up[0, 0], w_down[0, 0])
    summed = lax.psum_scatter(parts, "y", scatter_dimension=0, tiled=True)
    summed = whole(pieces_kernel, (PLACED, width), summed)
    back = lax.all_to_all(summed.reshape(LIVE, BLOCK, width), "z", 0, 0, tiled=True)
    y = whole(combine_kernel, x.shape, routes_t, gates_t, x, back.reshape(PLACED, width))
    sections = lax.axis_size("section")
    return lax.ppermute(y, "section", [(s, s + 1) for s in range(sections - 1)])[None]


def solution(mesh):
    sections, experts = mesh.devices.shape
    grid = Mesh(mesh.devices.reshape(sections, LIVE, experts // LIVE), ("section", "z", "y"))
    three = P("section", ("z", "y"), None)
    four = P("section", ("z", "y"), None, None)
    return jax.shard_map(
        shards,
        mesh=grid,
        in_specs=(three, three, three, four, four, four),
        out_specs=three,
        check_vma=False,
    )
```

```python
import functools

import jax
import jax.numpy as jnp
from jax import lax
from jax.experimental import pallas as pl
from jax.experimental.pallas import tpu as pltpu
from jax.sharding import Mesh, PartitionSpec as P


CAP = 10
LIVE = 8
PIECES = 4
BLOCK = CAP * PIECES
ROWS = LIVE * CAP
PLACED = LIVE * BLOCK
CHUNK = ROWS // 2
TERMS = 2

F32 = jnp.float32
BF16 = jnp.bfloat16
MIB = 1 << 20


def iota(shape, dim):
    return lax.broadcasted_iota(jnp.int32, shape, dim)


def slot_keys(routes_t):
    tokens = routes_t.shape[1]
    hit = jnp.concatenate(
        [jnp.max((routes_t == e).astype(F32), axis=0, keepdims=True) for e in range(LIVE)], axis=0
    )
    earlier = (iota((tokens, tokens), 0) < iota((tokens, tokens), 1)).astype(BF16)
    rank = jnp.dot(hit.astype(BF16), earlier, preferred_element_type=F32)
    return jnp.where(hit > 0, rank, -1.0)


def spread(values):
    pick = (iota((PLACED, LIVE), 0) // BLOCK == iota((PLACED, LIVE), 1)).astype(BF16)
    return jnp.dot(pick, values, preferred_element_type=F32)


def slot_match(routes_t):
    keys = spread(slot_keys(routes_t).astype(BF16))
    slots = (iota(keys.shape, 0) % CAP).astype(F32)
    return keys == slots


def piece_of(shape):
    return iota(shape, 0) // CAP % PIECES


def place_kernel(routes_ref, x_ref, out_ref):
    match = slot_match(routes_ref[...])
    piece = piece_of(match.shape)
    width = x_ref.shape[1] // PIECES
    total = jnp.zeros(out_ref.shape, F32)
    for p in range(PIECES):
        one = jnp.where(match & (piece == p), 1.0, 0.0).astype(BF16)
        total += jnp.dot(one, x_ref[:, p * width:(p + 1) * width], preferred_element_type=F32)
    out_ref[...] = total.astype(BF16)


def weights_kernel(routes_ref, gates_ref, out_ref):
    routes, gates = routes_ref[...], gates_ref[...]
    match = slot_match(routes)
    piece = piece_of(match.shape)
    rows = [
        jnp.sum(jnp.where(routes == e, gates, 0.0), axis=0, keepdims=True) for e in range(LIVE)
    ]
    left = jnp.concatenate(rows, axis=0)
    for t in range(TERMS):
        term = left.astype(BF16)
        left = left - term.astype(F32)
        full = jnp.where(match, spread(term), 0.0)
        for p in range(PIECES):
            out_ref[t, p] = jnp.where(piece == p, full, 0.0).T.astype(BF16)


def whole_rows_kernel(in_ref, *out_refs):
    width = in_ref.shape[1]
    row, col = iota((ROWS, PLACED), 0), iota((ROWS, PLACED), 1)
    same = (row // CAP == col // BLOCK) & (row % CAP == col % CAP)
    for p in range(PIECES):
        one = jnp.where(same & (col // CAP % PIECES == p), 1.0, 0.0).astype(BF16)
        moved = jnp.dot(one, in_ref[...], preferred_element_type=F32).astype(BF16)
        for c, out_ref in enumerate(out_refs):
            out_ref[:, p * width:(p + 1) * width] = moved[c * CHUNK:(c + 1) * CHUNK]


def pieces_kernel(*refs):
    *in_refs, out_ref = refs
    width = out_ref.shape[1]
    row, col = iota((PLACED, ROWS), 0), iota((PLACED, ROWS), 1)
    same = (col // CAP == row // BLOCK) & (col % CAP == row % CAP)
    total = jnp.zeros(out_ref.shape, F32)
    for p in range(PIECES):
        here = slice(p * width, (p + 1) * width)
        chunks = [
            sum(ref[:, here].astype(F32) for ref in in_refs[c:c + 3])
            for c in range(0, len(in_refs), 3)
        ]
        one = jnp.where(same & (row // CAP % PIECES == p), 1.0, 0.0).astype(BF16)
        rows = jnp.concatenate(chunks, axis=0).astype(BF16)
        total += jnp.dot(one, rows, preferred_element_type=F32)
    out_ref[...] = total.astype(BF16)


def expert_kernel(count, *refs):
    row_refs, (wg_ref, wu_ref, wd_ref) = refs[:count], refs[count:count + 3]
    out_refs, (rows_ref, both_ref) = refs[count + 3:2 * count + 3], refs[2 * count + 3:]
    hid = wg_ref.shape[1]
    both_ref[:, :hid] = wg_ref[...]
    both_ref[:, hid:] = wu_ref[...]
    for i, ref in enumerate(row_refs):
        rows_ref[i * CHUNK:(i + 1) * CHUNK] = ref[...]
    pre = jnp.dot(rows_ref[...], both_ref[...], preferred_element_type=F32)
    gate, up = pre[:, :hid], pre[:, hid:]
    act = (gate * jax.nn.sigmoid(gate) * up).astype(BF16)
    width = wd_ref.shape[1] // PIECES
    for p in range(PIECES):
        here = slice(p * width, (p + 1) * width)
        part = jnp.dot(act, wd_ref[:, here], preferred_element_type=F32).astype(BF16)
        for i, ref in enumerate(out_refs):
            ref[:, here] = part[i * CHUNK:(i + 1) * CHUNK]


def combine_kernel(weights_ref, x_ref, back_ref, out_ref):
    width = back_ref.shape[1]
    back = back_ref[...]
    for p in range(PIECES):
        here = slice(p * width, (p + 1) * width)
        total = x_ref[:, here].astype(F32)
        for t in range(TERMS):
            total += jnp.dot(weights_ref[t, p], back, preferred_element_type=F32)
        out_ref[:, here] = total.astype(BF16)


def local(kernel, shapes, *args, flops=0, scratch=(), limit=12 * MIB):
    shapes = [jax.ShapeDtypeStruct(shape, BF16) for shape in shapes]
    moved = sum(a.size * a.dtype.itemsize for a in [*args, *shapes])
    in_vmem = pl.BlockSpec(memory_space=pltpu.VMEM)
    return pl.pallas_call(
        kernel,
        out_shape=shapes,
        in_specs=[in_vmem] * len(args),
        out_specs=[in_vmem] * len(shapes),
        scratch_shapes=list(scratch),
        compiler_params=pltpu.CompilerParams(vmem_limit_bytes=limit),
        cost_estimate=pl.CostEstimate(flops=flops, bytes_accessed=moved, transcendentals=0),
    )(*args)


def expert_block(chunks, wg, wu, wd):
    depth, hid = wg.shape
    rows = CHUNK * len(chunks)
    return local(
        functools.partial(expert_kernel, len(chunks)),
        [c.shape for c in chunks],
        *chunks, wg, wu, wd,
        flops=6 * rows * depth * hid,
        scratch=[pltpu.VMEM((rows, depth), BF16), pltpu.VMEM((depth, 2 * hid), BF16)],
        limit=24 * MIB,
    )


def shifted(value, step):
    count = lax.axis_size("y")
    return lax.ppermute(value, "y", [(i, (i + step) % count) for i in range(count)])


def plus(moving, part):
    return (moving.astype(F32) + part.astype(F32)).astype(BF16)


def shards(x_fwd, routes_fwd, gates_fwd, w_gate, w_up, w_down):
    x = x_fwd[0]
    routes_t, gates_t = routes_fwd[0].T, gates_fwd[0].T
    depth = x.shape[1]
    width = depth // PIECES
    group = lax.axis_size("y")
    half = group // 2
    (placed,) = local(place_kernel, [(PLACED, width)], routes_t, x)
    arrived = lax.all_to_all(placed.reshape(LIVE, BLOCK, width), "z", 0, 0, tiled=True)
    own = local(
        whole_rows_kernel, [(CHUNK, depth)] * 2, arrived.reshape(PLACED, width)
    )

    reach = {(0, 1): half, (0, -1): half - 1, (1, 1): half - 1, (1, -1): half}
    streams = ((0, 1), (1, -1), (1, 1), (0, -1))
    held = {(c, 0): own[c] for c in range(2)}
    for hop in range(1, half + 1):
        for c, step in streams:
            if hop <= reach[c, step]:
                held[c, -step * hop] = shifted(held[c, -step * (hop - 1)], step)

    wg, wu, wd = w_gate[0, 0], w_up[0, 0], w_down[0, 0]
    near = [key for key in held if abs(key[1]) < half - 1]
    far = [key for key in held if abs(key[1]) >= half - 1]
    parts = {}
    parts.update(zip(near, expert_block([held[key] for key in near], wg, wu, wd)))
    wg, parts[0, 0] = lax.optimization_barrier((wg, parts[0, 0]))
    parts.update(zip(far, expert_block([held[key] for key in far], wg, wu, wd)))

    moving = {}
    for hop in range(half, 0, -1):
        for c, step in streams:
            if hop == reach[c, step]:
                far_part = (c, step * hop) if (c, step * hop) in parts else (c, -step * hop)
                moving[c, step] = shifted(parts[far_part], step)
            elif hop < reach[c, step]:
                moving[c, step] = shifted(plus(moving[c, step], parts[c, step * hop]), step)
    terms = []
    for c in range(2):
        terms += [parts[c, 0], moving[c, 1], moving[c, -1]]
    (summed,) = local(pieces_kernel, [(PLACED, width)], *terms)

    back = lax.all_to_all(summed.reshape(LIVE, BLOCK, width), "z", 0, 0, tiled=True)
    (weights,) = local(weights_kernel, [(TERMS, PIECES, x.shape[0], PLACED)], routes_t, gates_t)
    (y,) = local(combine_kernel, [x.shape], weights, x, back.reshape(PLACED, width))
    sections = lax.axis_size("section")
    return lax.ppermute(y, "section", [(s, s + 1) for s in range(sections - 1)])[None]


def solution(mesh):
    sections, experts = mesh.devices.shape
    grid = Mesh(mesh.devices.reshape(sections, LIVE, experts // LIVE), ("section", "z", "y"))
    three = P("section", ("z", "y"), None)
    four = P("section", ("z", "y"), None, None)
    return jax.shard_map(
        shards,
        mesh=grid,
        in_specs=(three, three, three, four, four, four),
        out_specs=three,
        check_vma=False,
    )
```

```python
import functools

import jax
import jax.numpy as jnp
from jax import lax
from jax.experimental import pallas as pl
from jax.experimental.pallas import tpu as pltpu
from jax.sharding import Mesh, PartitionSpec as P


CAP = 10
LIVE = 8
PIECES = 4
BLOCK = CAP * PIECES
ROWS = LIVE * CAP
PLACED = LIVE * BLOCK
CHUNK = ROWS // 2
TERMS = 2

F32 = jnp.float32
BF16 = jnp.bfloat16
MIB = 1 << 20


def iota(shape, dim):
    return lax.broadcasted_iota(jnp.int32, shape, dim)


def slot_keys(routes_t):
    tokens = routes_t.shape[1]
    hit = jnp.concatenate(
        [jnp.max((routes_t == e).astype(F32), axis=0, keepdims=True) for e in range(LIVE)], axis=0
    )
    earlier = (iota((tokens, tokens), 0) < iota((tokens, tokens), 1)).astype(BF16)
    rank = jnp.dot(hit.astype(BF16), earlier, preferred_element_type=F32)
    return jnp.where(hit > 0, rank, -1.0)


def spread(values):
    pick = (iota((PLACED, LIVE), 0) // BLOCK == iota((PLACED, LIVE), 1)).astype(BF16)
    return jnp.dot(pick, values, preferred_element_type=F32)


def slot_match(routes_t):
    keys = spread(slot_keys(routes_t).astype(BF16))
    slots = (iota(keys.shape, 0) % CAP).astype(F32)
    return keys == slots


def piece_of(shape):
    return iota(shape, 0) // CAP % PIECES


def place_kernel(routes_ref, gates_ref, x_ref, out_ref, tokens_ref):
    routes = routes_ref[...]
    match = slot_match(routes)
    piece = piece_of(match.shape)
    count, depth = x_ref.shape
    width = depth // PIECES
    total = jnp.zeros(out_ref.shape, F32)
    for p in range(PIECES):
        one = jnp.where(match & (piece == p), 1.0, 0.0).astype(BF16)
        total += jnp.dot(one, x_ref[:, p * width:(p + 1) * width], preferred_element_type=F32)
    out_ref[...] = total.astype(BF16)
    tokens_ref[:count] = x_ref[...]
    side = [routes.astype(F32).astype(BF16)]
    left = gates_ref[...]
    for _ in range(TERMS):
        side.append(left.astype(BF16))
        left = left - side[-1].astype(F32)
    side.append(jnp.zeros((routes.shape[0], depth - (TERMS + 1) * count), BF16))
    tokens_ref[count:] = jnp.concatenate(side, axis=1)


def weights_kernel(tokens_ref, out_ref):
    count = out_ref.shape[2]
    side = tokens_ref[count:, :(TERMS + 1) * count].astype(F32)
    routes = side[:, :count].astype(jnp.int32)
    match = slot_match(routes)
    piece = piece_of(match.shape)
    for t in range(TERMS):
        gates = side[:, (t + 1) * count:(t + 2) * count]
        rows = [
            jnp.sum(jnp.where(routes == e, gates, 0.0), axis=0, keepdims=True) for e in range(LIVE)
        ]
        full = jnp.where(match, spread(jnp.concatenate(rows, axis=0).astype(BF16)), 0.0)
        for p in range(PIECES):
            out_ref[t, p] = jnp.where(piece == p, full, 0.0).T.astype(BF16)


def whole_rows_kernel(in_ref, *out_refs):
    width = in_ref.shape[1]
    row, col = iota((ROWS, PLACED), 0), iota((ROWS, PLACED), 1)
    same = (row // CAP == col // BLOCK) & (row % CAP == col % CAP)
    for p in range(PIECES):
        one = jnp.where(same & (col // CAP % PIECES == p), 1.0, 0.0).astype(BF16)
        moved = jnp.dot(one, in_ref[...], preferred_element_type=F32).astype(BF16)
        for c, out_ref in enumerate(out_refs):
            out_ref[:, p * width:(p + 1) * width] = moved[c * CHUNK:(c + 1) * CHUNK]


def pieces_kernel(own_ref, *refs):
    *in_refs, out_ref = refs
    width = out_ref.shape[1]
    row, col = iota((PLACED, ROWS), 0), iota((PLACED, ROWS), 1)
    same = (col // CAP == row // BLOCK) & (col % CAP == row % CAP)
    total = jnp.zeros(out_ref.shape, F32)
    for p in range(PIECES):
        here = slice(p * width, (p + 1) * width)
        rows = own_ref[:, here].astype(F32) + jnp.concatenate(
            [
                in_refs[c][:, here].astype(F32) + in_refs[c + 1][:, here].astype(F32)
                for c in range(0, len(in_refs), 2)
            ],
            axis=0,
        )
        one = jnp.where(same & (row // CAP % PIECES == p), 1.0, 0.0).astype(BF16)
        total += jnp.dot(one, rows.astype(BF16), preferred_element_type=F32)
    out_ref[...] = total.astype(BF16)


def expert_kernel(count, *refs):
    row_refs, (wg_ref, wu_ref, wd_ref) = refs[:count], refs[count:count + 3]
    out_refs, (rows_ref, both_ref) = refs[count + 3:-2], refs[-2:]
    hid = wg_ref.shape[1]
    both_ref[:, :hid] = wg_ref[...]
    both_ref[:, hid:] = wu_ref[...]
    for i, ref in enumerate(row_refs):
        rows_ref[i * CHUNK:(i + 1) * CHUNK] = ref[...]
    pre = jnp.dot(rows_ref[...], both_ref[...], preferred_element_type=F32)
    gate, up = pre[:, :hid], pre[:, hid:]
    act = (gate * jax.nn.sigmoid(gate) * up).astype(BF16)
    width = wd_ref.shape[1] // PIECES
    for p in range(PIECES):
        here = slice(p * width, (p + 1) * width)
        part = jnp.dot(act, wd_ref[:, here], preferred_element_type=F32).astype(BF16)
        at = 0
        for ref in out_refs:
            ref[:, here] = part[at:at + ref.shape[0]]
            at += ref.shape[0]


def combine_kernel(weights_ref, tokens_ref, back_ref, out_ref):
    count, width = out_ref.shape[0], back_ref.shape[1]
    back = back_ref[...]
    for p in range(PIECES):
        here = slice(p * width, (p + 1) * width)
        total = tokens_ref[:count, here].astype(F32)
        for t in range(TERMS):
            total += jnp.dot(weights_ref[t, p], back, preferred_element_type=F32)
        out_ref[:, here] = total.astype(BF16)


def local(kernel, shapes, *args, flops=0, scratch=(), limit=12 * MIB):
    shapes = [jax.ShapeDtypeStruct(shape, BF16) for shape in shapes]
    moved = sum(a.size * a.dtype.itemsize for a in [*args, *shapes])
    in_vmem = pl.BlockSpec(memory_space=pltpu.VMEM)
    return pl.pallas_call(
        kernel,
        out_shape=shapes,
        in_specs=[in_vmem] * len(args),
        out_specs=[in_vmem] * len(shapes),
        scratch_shapes=list(scratch),
        compiler_params=pltpu.CompilerParams(vmem_limit_bytes=limit),
        cost_estimate=pl.CostEstimate(flops=flops, bytes_accessed=moved, transcendentals=0),
    )(*args)


def expert_block(chunks, heights, wg, wu, wd):
    depth, hid = wg.shape
    rows = CHUNK * len(chunks)
    return local(
        functools.partial(expert_kernel, len(chunks)),
        [(height, depth) for height in heights],
        *chunks, wg, wu, wd,
        flops=6 * rows * depth * hid,
        scratch=[pltpu.VMEM((rows, depth), BF16), pltpu.VMEM((depth, 2 * hid), BF16)],
        limit=24 * MIB,
    )


def shifted(value, step):
    count = lax.axis_size("y")
    return lax.ppermute(value, "y", [(i, (i + step) % count) for i in range(count)])


def reach_of(half):
    return {(0, 1): half, (0, -1): half - 1, (1, 1): half - 1, (1, -1): half}


def shifted_on(value, step=0):
    sections, count = lax.axis_size("section"), lax.axis_size("y")
    pairs = [
        (s * count + i, (s + 1) * count + (i + step) % count)
        for s in range(sections - 1)
        for i in range(count)
    ]
    return lax.ppermute(value, ("section", "y"), pairs)


def plus(moving, part):
    return (moving.astype(F32) + part.astype(F32)).astype(BF16)


def shards(x_fwd, routes_fwd, gates_fwd, w_gate, w_up, w_down):
    x = x_fwd[0]
    routes_t, gates_t = routes_fwd[0].T, gates_fwd[0].T
    topk = routes_t.shape[0]
    count, depth = x.shape
    width = depth // PIECES
    half = lax.axis_size("y") // 2
    placed, tokens = local(
        place_kernel, [(PLACED, width), (count + topk, depth)], routes_t, gates_t, x
    )
    arrived = lax.all_to_all(placed.reshape(LIVE, BLOCK, width), "z", 0, 0, tiled=True)
    own = local(
        whole_rows_kernel, [(CHUNK, depth)] * 2, arrived.reshape(PLACED, width)
    )

    reach = reach_of(half)
    streams = ((0, 1), (1, -1), (1, 1), (0, -1))
    held = {(c, 0): own[c] for c in range(2)}
    for hop in range(1, half + 1):
        for c, step in streams:
            if hop <= reach[c, step]:
                held[c, -step * hop] = shifted(held[c, -step * (hop - 1)], step)
    tokens = shifted_on(tokens)

    wg, wu, wd = w_gate[0, 0], w_up[0, 0], w_down[0, 0]
    near = [key for key in held if 0 < abs(key[1]) < half - 1]
    far = [key for key in held if abs(key[1]) >= half - 1]
    own_part, *near_parts = expert_block(
        [*own, *(held[key] for key in near)], [ROWS] + [CHUNK] * len(near), wg, wu, wd
    )
    parts = dict(zip(near, near_parts))
    wg, own_part = lax.optimization_barrier((wg, own_part))
    far_parts = expert_block([held[key] for key in far], [CHUNK] * len(far), wg, wu, wd)
    parts.update(zip(far, far_parts))
    own_part = shifted_on(own_part)

    moving = {}
    for hop in range(half, 0, -1):
        for c, step in streams:
            if hop == reach[c, step]:
                far_part = (c, step * hop) if (c, step * hop) in parts else (c, -step * hop)
                moving[c, step] = parts[far_part]
            elif hop < reach[c, step]:
                moving[c, step] = plus(moving[c, step], parts[c, step * hop])
            else:
                continue
            if hop > 1:
                moving[c, step] = shifted(moving[c, step], step)
            else:
                moving[c, step] = shifted_on(moving[c, step], step)
    sums = [moving[c, step] for c in range(2) for step in (1, -1)]
    (summed,) = local(pieces_kernel, [(PLACED, width)], own_part, *sums)

    back = lax.all_to_all(summed.reshape(LIVE, BLOCK, width), "z", 0, 0, tiled=True)
    (weights,) = local(weights_kernel, [(TERMS, PIECES, count, PLACED)], tokens)
    (y,) = local(combine_kernel, [x.shape], weights, tokens, back.reshape(PLACED, width))
    return y[None]


def solution(mesh):
    sections, experts = mesh.devices.shape
    grid = Mesh(mesh.devices.reshape(sections, LIVE, experts // LIVE), ("section", "z", "y"))
    three = P("section", ("z", "y"), None)
    four = P("section", ("z", "y"), None, None)

    return jax.shard_map(
        shards,
        mesh=grid,
        in_specs=(three, three, three, four, four, four),
        out_specs=three,
        check_vma=False,
    )
```

```python
import functools

import jax
import jax.numpy as jnp
from jax import lax
from jax.experimental import pallas as pl
from jax.experimental.pallas import tpu as pltpu
from jax.sharding import Mesh, PartitionSpec as P


CAP = 10
LIVE = 8
PIECES = 4
BLOCK = CAP * PIECES
ROWS = LIVE * CAP
PLACED = LIVE * BLOCK
CHUNK = ROWS // 2
TERMS = 2

F32 = jnp.float32
BF16 = jnp.bfloat16
MIB = 1 << 20


def iota(shape, dim):
    return lax.broadcasted_iota(jnp.int32, shape, dim)


def slot_keys(routes_t):
    tokens = routes_t.shape[1]
    hit = jnp.concatenate(
        [jnp.max((routes_t == e).astype(F32), axis=0, keepdims=True) for e in range(LIVE)], axis=0
    )
    earlier = (iota((tokens, tokens), 0) < iota((tokens, tokens), 1)).astype(BF16)
    rank = jnp.dot(hit.astype(BF16), earlier, preferred_element_type=F32)
    return jnp.where(hit > 0, rank, -1.0)


def spread(values):
    pick = (iota((PLACED, LIVE), 0) // BLOCK == iota((PLACED, LIVE), 1)).astype(BF16)
    return jnp.dot(pick, values, preferred_element_type=F32)


def slot_match(routes_t):
    keys = spread(slot_keys(routes_t).astype(BF16))
    slots = (iota(keys.shape, 0) % CAP).astype(F32)
    return keys == slots


def piece_of(shape):
    return iota(shape, 0) // CAP % PIECES


def place_kernel(routes_ref, x_ref, out_ref):
    match = slot_match(routes_ref[...])
    piece = piece_of(match.shape)
    width = x_ref.shape[1] // PIECES
    total = jnp.zeros(out_ref.shape, F32)
    for p in range(PIECES):
        one = jnp.where(match & (piece == p), 1.0, 0.0).astype(BF16)
        total += jnp.dot(one, x_ref[:, p * width:(p + 1) * width], preferred_element_type=F32)
    out_ref[...] = total.astype(BF16)


def weights_kernel(routes_ref, gates_ref, out_ref):
    routes, gates = routes_ref[...], gates_ref[...]
    match = slot_match(routes)
    piece = piece_of(match.shape)
    rows = [
        jnp.sum(jnp.where(routes == e, gates, 0.0), axis=0, keepdims=True) for e in range(LIVE)
    ]
    left = jnp.concatenate(rows, axis=0)
    for t in range(TERMS):
        term = left.astype(BF16)
        left = left - term.astype(F32)
        full = jnp.where(match, spread(term), 0.0)
        for p in range(PIECES):
            out_ref[t, p] = jnp.where(piece == p, full, 0.0).T.astype(BF16)


def whole_rows_kernel(in_ref, *out_refs):
    width = in_ref.shape[1]
    row, col = iota((ROWS, PLACED), 0), iota((ROWS, PLACED), 1)
    same = (row // CAP == col // BLOCK) & (row % CAP == col % CAP)
    for p in range(PIECES):
        one = jnp.where(same & (col // CAP % PIECES == p), 1.0, 0.0).astype(BF16)
        moved = jnp.dot(one, in_ref[...], preferred_element_type=F32).astype(BF16)
        for c, out_ref in enumerate(out_refs):
            out_ref[:, p * width:(p + 1) * width] = moved[c * CHUNK:(c + 1) * CHUNK]


def pieces_kernel(*refs):
    *in_refs, out_ref = refs
    width = out_ref.shape[1]
    row, col = iota((PLACED, ROWS), 0), iota((PLACED, ROWS), 1)
    same = (col // CAP == row // BLOCK) & (col % CAP == row % CAP)
    total = jnp.zeros(out_ref.shape, F32)
    for p in range(PIECES):
        here = slice(p * width, (p + 1) * width)
        chunks = [
            sum(ref[:, here].astype(F32) for ref in in_refs[c:c + 3])
            for c in range(0, len(in_refs), 3)
        ]
        one = jnp.where(same & (row // CAP % PIECES == p), 1.0, 0.0).astype(BF16)
        rows = jnp.concatenate(chunks, axis=0).astype(BF16)
        total += jnp.dot(one, rows, preferred_element_type=F32)
    out_ref[...] = total.astype(BF16)


def expert_kernel(count, *refs):
    row_refs, (wg_ref, wu_ref, wd_ref) = refs[:count], refs[count:count + 3]
    out_refs, (rows_ref, both_ref) = refs[count + 3:2 * count + 3], refs[2 * count + 3:]
    hid = wg_ref.shape[1]
    both_ref[:, :hid] = wg_ref[...]
    both_ref[:, hid:] = wu_ref[...]
    for i, ref in enumerate(row_refs):
        rows_ref[i * CHUNK:(i + 1) * CHUNK] = ref[...]
    pre = jnp.dot(rows_ref[...], both_ref[...], preferred_element_type=F32)
    gate, up = pre[:, :hid], pre[:, hid:]
    act = (gate * jax.nn.sigmoid(gate) * up).astype(BF16)
    width = wd_ref.shape[1] // PIECES
    for p in range(PIECES):
        here = slice(p * width, (p + 1) * width)
        part = jnp.dot(act, wd_ref[:, here], preferred_element_type=F32).astype(BF16)
        for i, ref in enumerate(out_refs):
            ref[:, here] = part[i * CHUNK:(i + 1) * CHUNK]


def combine_kernel(weights_ref, x_ref, back_ref, out_ref):
    width = back_ref.shape[1]
    back = back_ref[...]
    for p in range(PIECES):
        here = slice(p * width, (p + 1) * width)
        total = x_ref[:, here].astype(F32)
        for t in range(TERMS):
            total += jnp.dot(weights_ref[t, p], back, preferred_element_type=F32)
        out_ref[:, here] = total.astype(BF16)


def local(kernel, shapes, *args, flops=0, scratch=(), limit=12 * MIB):
    shapes = [jax.ShapeDtypeStruct(shape, BF16) for shape in shapes]
    moved = sum(a.size * a.dtype.itemsize for a in [*args, *shapes])
    in_vmem = pl.BlockSpec(memory_space=pltpu.VMEM)
    return pl.pallas_call(
        kernel,
        out_shape=shapes,
        in_specs=[in_vmem] * len(args),
        out_specs=[in_vmem] * len(shapes),
        scratch_shapes=list(scratch),
        compiler_params=pltpu.CompilerParams(vmem_limit_bytes=limit),
        cost_estimate=pl.CostEstimate(flops=flops, bytes_accessed=moved, transcendentals=0),
    )(*args)


def expert_block(chunks, wg, wu, wd):
    depth, hid = wg.shape
    rows = CHUNK * len(chunks)
    return local(
        functools.partial(expert_kernel, len(chunks)),
        [c.shape for c in chunks],
        *chunks, wg, wu, wd,
        flops=6 * rows * depth * hid,
        scratch=[pltpu.VMEM((rows, depth), BF16), pltpu.VMEM((depth, 2 * hid), BF16)],
        limit=24 * MIB,
    )


def shifted(value, step):
    count = lax.axis_size("y")
    return lax.ppermute(value, "y", [(i, (i + step) % count) for i in range(count)])


def reach_of(half):
    return {(0, 1): half, (0, -1): half - 1, (1, 1): half - 1, (1, -1): half}


def plus(moving, part):
    return (moving.astype(F32) + part.astype(F32)).astype(BF16)


def shards(x_fwd, routes_fwd, gates_fwd, w_gate, w_up, w_down):
    x = x_fwd[0]
    routes_t, gates_t = routes_fwd[0].T, gates_fwd[0].T
    depth = x.shape[1]
    width = depth // PIECES
    group = lax.axis_size("y")
    half = group // 2
    (placed,) = local(place_kernel, [(PLACED, width)], routes_t, x)
    arrived = lax.all_to_all(placed.reshape(LIVE, BLOCK, width), "z", 0, 0, tiled=True)
    own = local(
        whole_rows_kernel, [(CHUNK, depth)] * 2, arrived.reshape(PLACED, width)
    )

    reach = reach_of(half)
    streams = ((0, 1), (1, -1), (1, 1), (0, -1))
    held = {(c, 0): own[c] for c in range(2)}
    for hop in range(1, half + 1):
        for c, step in streams:
            if hop <= reach[c, step]:
                held[c, -step * hop] = shifted(held[c, -step * (hop - 1)], step)

    wg, wu, wd = w_gate[0, 0], w_up[0, 0], w_down[0, 0]
    near = [key for key in held if abs(key[1]) < half]
    far = [key for key in held if abs(key[1]) == half]
    parts = {}
    parts.update(zip(near, expert_block([held[key] for key in near], wg, wu, wd)))
    wg, parts[0, 0] = lax.optimization_barrier((wg, parts[0, 0]))
    parts.update(zip(far, expert_block([held[key] for key in far], wg, wu, wd)))

    moving = {}
    for hop in range(half, 0, -1):
        for c, step in streams:
            if hop == reach[c, step]:
                far_part = (c, step * hop) if (c, step * hop) in parts else (c, -step * hop)
                moving[c, step] = shifted(parts[far_part], step)
            elif hop < reach[c, step]:
                total = plus(moving[c, step], parts[c, step * hop])
                moving[c, step] = shifted(total, step)
    terms = []
    for c in range(2):
        terms += [parts[c, 0], moving[c, 1], moving[c, -1]]
    (summed,) = local(pieces_kernel, [(PLACED, width)], *terms)

    back = lax.all_to_all(summed.reshape(LIVE, BLOCK, width), "z", 0, 0, tiled=True)
    (weights,) = local(weights_kernel, [(TERMS, PIECES, x.shape[0], PLACED)], routes_t, gates_t)
    (y,) = local(combine_kernel, [x.shape], weights, x, back.reshape(PLACED, width))
    sections = lax.axis_size("section")
    return lax.ppermute(y, "section", [(s, s + 1) for s in range(sections - 1)])[None]


def solution(mesh):
    sections, experts = mesh.devices.shape
    grid = Mesh(mesh.devices.reshape(sections, LIVE, experts // LIVE), ("section", "z", "y"))
    three = P("section", ("z", "y"), None)
    four = P("section", ("z", "y"), None, None)

    return jax.shard_map(
        shards,
        mesh=grid,
        in_specs=(three, three, three, four, four, four),
        out_specs=three,
        check_vma=False,
    )
```

```python
import functools

import jax
import jax.numpy as jnp
from jax import lax
from jax.experimental import pallas as pl
from jax.experimental.pallas import tpu as pltpu
from jax.sharding import Mesh, PartitionSpec as P


CAP = 10
LIVE = 8
PIECES = 4
BLOCK = CAP * PIECES
ROWS = LIVE * CAP
PLACED = LIVE * BLOCK
CHUNK = ROWS // 2
TERMS = 2

F32 = jnp.float32
BF16 = jnp.bfloat16
MIB = 1 << 20


def iota(shape, dim):
    return lax.broadcasted_iota(jnp.int32, shape, dim)


def slot_keys(routes_t):
    tokens = routes_t.shape[1]
    hit = jnp.concatenate(
        [jnp.max((routes_t == e).astype(F32), axis=0, keepdims=True) for e in range(LIVE)], axis=0
    )
    earlier = (iota((tokens, tokens), 0) < iota((tokens, tokens), 1)).astype(BF16)
    rank = jnp.dot(hit.astype(BF16), earlier, preferred_element_type=F32)
    return jnp.where(hit > 0, rank, -1.0)


def spread(values):
    pick = (iota((PLACED, LIVE), 0) // BLOCK == iota((PLACED, LIVE), 1)).astype(BF16)
    return jnp.dot(pick, values, preferred_element_type=F32)


def slot_match(routes_t):
    keys = spread(slot_keys(routes_t).astype(BF16))
    slots = (iota(keys.shape, 0) % CAP).astype(F32)
    return keys == slots


def piece_of(shape):
    return iota(shape, 0) // CAP % PIECES


def place_kernel(routes_hbm, gates_hbm, x_hbm, out_ref, tokens_ref, routes_ref, gates_ref, sems):
    count, depth = x_hbm.shape
    width = depth // PIECES
    copies = [
        pltpu.make_async_copy(routes_hbm, routes_ref, sems.at[0]),
        pltpu.make_async_copy(x_hbm, tokens_ref.at[:count], sems.at[1]),
        pltpu.make_async_copy(gates_hbm, gates_ref, sems.at[2]),
    ]
    for copy in copies:
        copy.start()
    copies[0].wait()
    routes = routes_ref[...]
    match = slot_match(routes)
    piece = piece_of(match.shape)
    ones = [jnp.where(match & (piece == p), 1.0, 0.0).astype(BF16) for p in range(PIECES)]
    copies[2].wait()
    side = [routes.astype(F32).astype(BF16)]
    left = gates_ref[...]
    for _ in range(TERMS):
        side.append(left.astype(BF16))
        left = left - side[-1].astype(F32)
    side.append(jnp.zeros((routes.shape[0], depth - (TERMS + 1) * count), BF16))
    tokens_ref[count:] = jnp.concatenate(side, axis=1)
    copies[1].wait()
    x = jnp.concatenate(
        [tokens_ref[:count, p * width:(p + 1) * width] for p in range(PIECES)], axis=0
    )
    out_ref[...] = jnp.dot(
        jnp.concatenate(ones, axis=1), x, preferred_element_type=F32
    ).astype(BF16)


def weights_kernel(tokens_ref, out_ref):
    count = out_ref.shape[2]
    side = tokens_ref[count:, :(TERMS + 1) * count].astype(F32)
    routes = side[:, :count].astype(jnp.int32)
    match = slot_match(routes)
    piece = piece_of(match.shape)
    for t in range(TERMS):
        gates = side[:, (t + 1) * count:(t + 2) * count]
        rows = [
            jnp.sum(jnp.where(routes == e, gates, 0.0), axis=0, keepdims=True) for e in range(LIVE)
        ]
        full = jnp.where(match, spread(jnp.concatenate(rows, axis=0).astype(BF16)), 0.0)
        for p in range(PIECES):
            out_ref[t, p] = jnp.where(piece == p, full, 0.0).T.astype(BF16)


def whole_rows_kernel(in_ref, *out_refs):
    width = in_ref.shape[1]
    row, col = iota((ROWS, PLACED), 0), iota((ROWS, PLACED), 1)
    same = (row // CAP == col // BLOCK) & (row % CAP == col % CAP)
    for p in range(PIECES):
        one = jnp.where(same & (col // CAP % PIECES == p), 1.0, 0.0).astype(BF16)
        moved = jnp.dot(one, in_ref[...], preferred_element_type=F32).astype(BF16)
        for c, out_ref in enumerate(out_refs):
            out_ref[:, p * width:(p + 1) * width] = moved[c * CHUNK:(c + 1) * CHUNK]


def pieces_kernel(own_ref, *refs):
    *in_refs, out_ref = refs
    width = out_ref.shape[1]
    rows = []
    for p in range(PIECES):
        here = slice(p * width, (p + 1) * width)
        for c in range(2):
            total = own_ref[c * CHUNK:(c + 1) * CHUNK, here].astype(F32)
            for ref in in_refs[2 * c:2 * c + 2]:
                total += ref[:, here].astype(F32)
            rows.append(total.astype(BF16))
    row, col = iota((PLACED, PLACED), 0), iota((PLACED, PLACED), 1)
    block, slot = col % ROWS // CAP, col % CAP
    same = row == block * BLOCK + col // ROWS * CAP + slot
    out_ref[...] = jnp.dot(
        jnp.where(same, 1.0, 0.0).astype(BF16),
        jnp.concatenate(rows, axis=0),
        preferred_element_type=F32,
    ).astype(BF16)


def expert_kernel(count, *refs):
    row_refs, (wg_ref, wu_ref, wd_ref) = refs[:count], refs[count:count + 3]
    out_refs, (rows_ref, both_ref) = refs[count + 3:-2], refs[-2:]
    hid = wg_ref.shape[1]
    both_ref[:, :hid] = wg_ref[...]
    both_ref[:, hid:] = wu_ref[...]
    for i, ref in enumerate(row_refs):
        rows_ref[i * CHUNK:(i + 1) * CHUNK] = ref[...]
    pre = jnp.dot(rows_ref[...], both_ref[...], preferred_element_type=F32)
    gate, up = pre[:, :hid], pre[:, hid:]
    act = (gate * jax.nn.sigmoid(gate) * up).astype(BF16)
    width = wd_ref.shape[1] // PIECES
    for p in range(PIECES):
        here = slice(p * width, (p + 1) * width)
        part = jnp.dot(act, wd_ref[:, here], preferred_element_type=F32).astype(BF16)
        at = 0
        for ref in out_refs:
            ref[:, here] = part[at:at + ref.shape[0]]
            at += ref.shape[0]


def combine_kernel(weights_ref, tokens_ref, back_ref, out_ref):
    count, width = out_ref.shape[0], back_ref.shape[1]
    back = back_ref[...]
    for p in range(PIECES):
        here = slice(p * width, (p + 1) * width)
        total = tokens_ref[:count, here].astype(F32)
        for t in range(TERMS):
            total += jnp.dot(weights_ref[t, p], back, preferred_element_type=F32)
        out_ref[:, here] = total.astype(BF16)


def local(kernel, shapes, *args, flops=0, scratch=(), limit=8 * MIB, space=pltpu.VMEM):
    shapes = [jax.ShapeDtypeStruct(shape, BF16) for shape in shapes]
    moved = sum(a.size * a.dtype.itemsize for a in [*args, *shapes])
    in_vmem = pl.BlockSpec(memory_space=pltpu.VMEM)
    return pl.pallas_call(
        kernel,
        out_shape=shapes,
        in_specs=[pl.BlockSpec(memory_space=space)] * len(args),
        out_specs=[in_vmem] * len(shapes),
        scratch_shapes=list(scratch),
        compiler_params=pltpu.CompilerParams(vmem_limit_bytes=limit),
        cost_estimate=pl.CostEstimate(flops=flops, bytes_accessed=moved, transcendentals=0),
    )(*args)


def expert_block(chunks, heights, wg, wu, wd):
    depth, hid = wg.shape
    rows = CHUNK * len(chunks)
    return local(
        functools.partial(expert_kernel, len(chunks)),
        [(height, depth) for height in heights],
        *chunks, wg, wu, wd,
        flops=6 * rows * depth * hid,
        scratch=[pltpu.VMEM((rows, depth), BF16), pltpu.VMEM((depth, 2 * hid), BF16)],
        limit=14 * MIB,
    )


def shifted(value, step):
    count = lax.axis_size("y")
    return lax.ppermute(value, "y", [(i, (i + step) % count) for i in range(count)])


def reach_of(half):
    return {(0, 1): half, (0, -1): half - 1, (1, 1): half - 1, (1, -1): half}


def shifted_on(value):
    sections = lax.axis_size("section")
    return lax.ppermute(value, "section", [(i, i + 1) for i in range(sections - 1)])


def plus(moving, part):
    return (moving.astype(F32) + part.astype(F32)).astype(BF16)


def shards(x_fwd, routes_fwd, gates_fwd, w_gate, w_up, w_down):
    x = x_fwd[0]
    routes_t, gates_t = routes_fwd[0].T, gates_fwd[0].T
    topk = routes_t.shape[0]
    count, depth = x.shape
    width = depth // PIECES
    half = lax.axis_size("y") // 2
    placed, tokens = local(
        place_kernel,
        [(PLACED, width), (count + topk, depth)],
        routes_t, gates_t, x,
        scratch=[
            pltpu.VMEM((topk, count), jnp.int32),
            pltpu.VMEM((topk, count), F32),
            pltpu.SemaphoreType.DMA((3,)),
        ],
        space=pltpu.HBM,
        limit=62 * MIB,
    )
    tokens = shifted_on(tokens)
    arrived = lax.all_to_all(placed.reshape(LIVE, BLOCK, width), "z", 0, 0, tiled=True)
    own = local(
        whole_rows_kernel, [(CHUNK, depth)] * 2, arrived.reshape(PLACED, width)
    )

    reach = reach_of(half)
    streams = ((0, 1), (1, -1), (1, 1), (0, -1))
    held = {(c, 0): own[c] for c in range(2)}
    for hop in range(1, half + 1):
        for c, step in streams:
            if hop <= reach[c, step]:
                held[c, -step * hop] = shifted(held[c, -step * (hop - 1)], step)

    wg, wu, wd = w_gate[0, 0], w_up[0, 0], w_down[0, 0]
    near = [key for key in held if 0 < abs(key[1]) < half - 1]
    far = [key for key in held if abs(key[1]) >= half - 1]
    own_part, *near_parts = expert_block(
        [*own, *(held[key] for key in near)], [ROWS] + [CHUNK] * len(near), wg, wu, wd
    )
    parts = dict(zip(near, near_parts))
    wg, own_part = lax.optimization_barrier((wg, own_part))
    far_parts = expert_block([held[key] for key in far], [CHUNK] * len(far), wg, wu, wd)
    parts.update(zip(far, far_parts))

    moving = {}
    for hop in range(half, 0, -1):
        for c, step in streams:
            if hop == reach[c, step]:
                far_part = (c, step * hop) if (c, step * hop) in parts else (c, -step * hop)
                moving[c, step] = parts[far_part]
            elif hop < reach[c, step]:
                moving[c, step] = plus(moving[c, step], parts[c, step * hop])
            else:
                continue
            moving[c, step] = shifted(moving[c, step], step)
    sums = [moving[c, step] for c in range(2) for step in (1, -1)]
    (summed,) = local(pieces_kernel, [(PLACED, width)], own_part, *sums)
    summed = shifted_on(summed)

    back = lax.all_to_all(summed.reshape(LIVE, BLOCK, width), "z", 0, 0, tiled=True)
    (weights,) = local(weights_kernel, [(TERMS, PIECES, count, PLACED)], tokens)
    (y,) = local(combine_kernel, [x.shape], weights, tokens, back.reshape(PLACED, width))
    return y[None]


def solution(mesh):
    sections, experts = mesh.devices.shape
    grid = Mesh(mesh.devices.reshape(sections, LIVE, experts // LIVE), ("section", "z", "y"))
    three = P("section", ("z", "y"), None)
    four = P("section", ("z", "y"), None, None)

    return jax.shard_map(
        shards,
        mesh=grid,
        in_specs=(three, three, three, four, four, four),
        out_specs=three,
        check_vma=False,
    )
```

```python
import functools

import jax
import jax.numpy as jnp
from jax import lax
from jax.experimental import pallas as pl
from jax.experimental.pallas import tpu as pltpu
from jax.sharding import Mesh, PartitionSpec as P


CAP = 10
LIVE = 8
PIECES = 4
BLOCK = CAP * PIECES
ROWS = LIVE * CAP
PLACED = LIVE * BLOCK
CHUNK = ROWS // 2
TERMS = 2

F32 = jnp.float32
BF16 = jnp.bfloat16
MIB = 1 << 20


def iota(shape, dim):
    return lax.broadcasted_iota(jnp.int32, shape, dim)


def slot_keys(routes_t):
    tokens = routes_t.shape[1]
    hit = jnp.concatenate(
        [jnp.max((routes_t == e).astype(F32), axis=0, keepdims=True) for e in range(LIVE)], axis=0
    )
    earlier = (iota((tokens, tokens), 0) < iota((tokens, tokens), 1)).astype(BF16)
    rank = jnp.dot(hit.astype(BF16), earlier, preferred_element_type=F32)
    return jnp.where(hit > 0, rank, -1.0)


def spread(values):
    pick = (iota((PLACED, LIVE), 0) // BLOCK == iota((PLACED, LIVE), 1)).astype(BF16)
    return jnp.dot(pick, values, preferred_element_type=F32)


def slot_match(routes_t):
    keys = spread(slot_keys(routes_t).astype(BF16))
    slots = (iota(keys.shape, 0) % CAP).astype(F32)
    return keys == slots


def piece_of(shape):
    return iota(shape, 0) // CAP % PIECES


def place_kernel(routes_hbm, x_hbm, out_ref, routes_ref, x_ref, sems):
    width = x_ref.shape[1] // PIECES
    routes_copy = pltpu.make_async_copy(routes_hbm, routes_ref, sems.at[0])
    x_copy = pltpu.make_async_copy(x_hbm, x_ref, sems.at[1])
    routes_copy.start()
    x_copy.start()
    routes_copy.wait()
    match = slot_match(routes_ref[...])
    piece = piece_of(match.shape)
    ones = [jnp.where(match & (piece == p), 1.0, 0.0).astype(BF16) for p in range(PIECES)]
    x_copy.wait()
    x = jnp.concatenate([x_ref[:, p * width:(p + 1) * width] for p in range(PIECES)], axis=0)
    out_ref[...] = jnp.dot(
        jnp.concatenate(ones, axis=1), x, preferred_element_type=F32
    ).astype(BF16)


def weights_kernel(routes_ref, gates_ref, out_ref):
    routes, gates = routes_ref[...], gates_ref[...]
    match = slot_match(routes)
    piece = piece_of(match.shape)
    rows = [
        jnp.sum(jnp.where(routes == e, gates, 0.0), axis=0, keepdims=True) for e in range(LIVE)
    ]
    left = jnp.concatenate(rows, axis=0)
    for t in range(TERMS):
        term = left.astype(BF16)
        left = left - term.astype(F32)
        full = jnp.where(match, spread(term), 0.0)
        for p in range(PIECES):
            out_ref[t, p] = jnp.where(piece == p, full, 0.0).T.astype(BF16)


def whole_rows_kernel(in_ref, *out_refs):
    width = in_ref.shape[1]
    row, col = iota((ROWS, PLACED), 0), iota((ROWS, PLACED), 1)
    same = (row // CAP == col // BLOCK) & (row % CAP == col % CAP)
    for p in range(PIECES):
        one = jnp.where(same & (col // CAP % PIECES == p), 1.0, 0.0).astype(BF16)
        moved = jnp.dot(one, in_ref[...], preferred_element_type=F32).astype(BF16)
        for c, out_ref in enumerate(out_refs):
            out_ref[:, p * width:(p + 1) * width] = moved[c * CHUNK:(c + 1) * CHUNK]


def pieces_kernel(*refs):
    *in_refs, out_ref = refs
    width = out_ref.shape[1]
    rows = []
    for p in range(PIECES):
        here = slice(p * width, (p + 1) * width)
        for c in range(2):
            total = sum(ref[:, here].astype(F32) for ref in in_refs[3 * c:3 * c + 3])
            rows.append(total.astype(BF16))
    row, col = iota((PLACED, PLACED), 0), iota((PLACED, PLACED), 1)
    block, slot = col % ROWS // CAP, col % CAP
    same = row == block * BLOCK + col // ROWS * CAP + slot
    out_ref[...] = jnp.dot(
        jnp.where(same, 1.0, 0.0).astype(BF16),
        jnp.concatenate(rows, axis=0),
        preferred_element_type=F32,
    ).astype(BF16)


def expert_kernel(count, *refs):
    row_refs, (wg_ref, wu_ref, wd_ref) = refs[:count], refs[count:count + 3]
    out_refs, (rows_ref, both_ref) = refs[count + 3:2 * count + 3], refs[2 * count + 3:]
    hid = wg_ref.shape[1]
    both_ref[:, :hid] = wg_ref[...]
    both_ref[:, hid:] = wu_ref[...]
    for i, ref in enumerate(row_refs):
        rows_ref[i * CHUNK:(i + 1) * CHUNK] = ref[...]
    pre = jnp.dot(rows_ref[...], both_ref[...], preferred_element_type=F32)
    gate, up = pre[:, :hid], pre[:, hid:]
    act = (gate * jax.nn.sigmoid(gate) * up).astype(BF16)
    width = wd_ref.shape[1] // PIECES
    for p in range(PIECES):
        here = slice(p * width, (p + 1) * width)
        part = jnp.dot(act, wd_ref[:, here], preferred_element_type=F32).astype(BF16)
        for i, ref in enumerate(out_refs):
            ref[:, here] = part[i * CHUNK:(i + 1) * CHUNK]


def combine_kernel(weights_ref, x_ref, back_ref, out_ref):
    width = back_ref.shape[1]
    back = back_ref[...]
    for p in range(PIECES):
        here = slice(p * width, (p + 1) * width)
        total = x_ref[:, here].astype(F32)
        for t in range(TERMS):
            total += jnp.dot(weights_ref[t, p], back, preferred_element_type=F32)
        out_ref[:, here] = total.astype(BF16)


def local(kernel, shapes, *args, flops=0, scratch=(), limit=8 * MIB, space=pltpu.VMEM):
    shapes = [jax.ShapeDtypeStruct(shape, BF16) for shape in shapes]
    moved = sum(a.size * a.dtype.itemsize for a in [*args, *shapes])
    in_vmem = pl.BlockSpec(memory_space=pltpu.VMEM)
    return pl.pallas_call(
        kernel,
        out_shape=shapes,
        in_specs=[pl.BlockSpec(memory_space=space)] * len(args),
        out_specs=[in_vmem] * len(shapes),
        scratch_shapes=list(scratch),
        compiler_params=pltpu.CompilerParams(vmem_limit_bytes=limit),
        cost_estimate=pl.CostEstimate(flops=flops, bytes_accessed=moved, transcendentals=0),
    )(*args)


def expert_block(chunks, wg, wu, wd):
    depth, hid = wg.shape
    rows = CHUNK * len(chunks)
    return local(
        functools.partial(expert_kernel, len(chunks)),
        [c.shape for c in chunks],
        *chunks, wg, wu, wd,
        flops=6 * rows * depth * hid,
        scratch=[pltpu.VMEM((rows, depth), BF16), pltpu.VMEM((depth, 2 * hid), BF16)],
        limit=14 * MIB,
    )


def shifted(value, step):
    count = lax.axis_size("y")
    return lax.ppermute(value, "y", [(i, (i + step) % count) for i in range(count)])


def reach_of(half):
    return {(0, 1): half, (0, -1): half - 1, (1, 1): half - 1, (1, -1): half}


def plus(moving, part):
    return (moving.astype(F32) + part.astype(F32)).astype(BF16)


def shards(x_fwd, routes_fwd, gates_fwd, w_gate, w_up, w_down):
    x = x_fwd[0]
    routes_t, gates_t = routes_fwd[0].T, gates_fwd[0].T
    depth = x.shape[1]
    width = depth // PIECES
    group = lax.axis_size("y")
    half = group // 2
    (placed,) = local(
        place_kernel,
        [(PLACED, width)],
        routes_t, x,
        scratch=[
            pltpu.VMEM(routes_t.shape, jnp.int32),
            pltpu.VMEM(x.shape, BF16),
            pltpu.SemaphoreType.DMA((2,)),
        ],
        limit=62 * MIB,
        space=pltpu.HBM,
    )
    arrived = lax.all_to_all(placed.reshape(LIVE, BLOCK, width), "z", 0, 0, tiled=True)
    own = local(
        whole_rows_kernel, [(CHUNK, depth)] * 2, arrived.reshape(PLACED, width)
    )

    reach = reach_of(half)
    streams = ((0, 1), (1, -1), (1, 1), (0, -1))
    held = {(c, 0): own[c] for c in range(2)}
    for hop in range(1, half + 1):
        for c, step in streams:
            if hop <= reach[c, step]:
                held[c, -step * hop] = shifted(held[c, -step * (hop - 1)], step)

    wg, wu, wd = w_gate[0, 0], w_up[0, 0], w_down[0, 0]
    near = [key for key in held if abs(key[1]) < half]
    far = [key for key in held if abs(key[1]) == half]
    parts = {}
    parts.update(zip(near, expert_block([held[key] for key in near], wg, wu, wd)))
    wg, parts[0, 0] = lax.optimization_barrier((wg, parts[0, 0]))
    parts.update(zip(far, expert_block([held[key] for key in far], wg, wu, wd)))

    moving = {}
    for hop in range(half, 0, -1):
        for c, step in streams:
            if hop == reach[c, step]:
                far_part = (c, step * hop) if (c, step * hop) in parts else (c, -step * hop)
                moving[c, step] = shifted(parts[far_part], step)
            elif hop < reach[c, step]:
                total = plus(moving[c, step], parts[c, step * hop])
                moving[c, step] = shifted(total, step)
    terms = []
    for c in range(2):
        terms += [parts[c, 0], moving[c, 1], moving[c, -1]]
    (summed,) = local(pieces_kernel, [(PLACED, width)], *terms)

    back = lax.all_to_all(summed.reshape(LIVE, BLOCK, width), "z", 0, 0, tiled=True)
    (weights,) = local(weights_kernel, [(TERMS, PIECES, x.shape[0], PLACED)], routes_t, gates_t)
    (y,) = local(combine_kernel, [x.shape], weights, x, back.reshape(PLACED, width))
    sections = lax.axis_size("section")
    return lax.ppermute(y, "section", [(s, s + 1) for s in range(sections - 1)])[None]


def solution(mesh):
    sections, experts = mesh.devices.shape
    grid = Mesh(mesh.devices.reshape(sections, LIVE, experts // LIVE), ("section", "z", "y"))
    three = P("section", ("z", "y"), None)
    four = P("section", ("z", "y"), None, None)

    return jax.shard_map(
        shards,
        mesh=grid,
        in_specs=(three, three, three, four, four, four),
        out_specs=three,
        check_vma=False,
    )
```
